32 devices in a mesh: fs: 8 (over z, x), pol: 4 (over y, core).
Axes of the slice: x: 2, y: 2, z: 4, core: 2. Of those that a mesh axis runs over, the one named last changes fastest.
Arguments:
- facets: bfloat16 [4, 64, 4096, 128], P('pol', 'fs'), may hold values from -6 to 6
- owners: int32 [64], replicated, may hold values from 0 to 7, as said below
- counts: int32 [64], replicated, may hold values from 1 to 8, as said below
- coords: float32 [2, 128, 8, 128], P(None, 'fs'), may hold values from 0 to 512
- station_ids: int32 [128, 8, 2, 128], P('fs'), may hold values from 0 to 511
- jones_table: float32 [8, 512], replicated, may hold values from -3 to 3
Outputs:
- predicted: float32 [4, 2, 128, 8, 128], P('pol', None, 'fs')
The draws below stay inside these ranges and needn't reach their ends.
Inputs may be any that keep to these rules, and one draw needn't show every extreme that they name: `owners`: each fs index owns at most 16 subgrids, and some index owns exactly 16. `counts`: some subgrid has exactly 8 blocks.
All inputs are finite; a program needn't handle non-finite values.
Results may differ from the reference program's by a relative error of at most 0.0055.
Values may be sent and summed in bfloat16 or wider, within the bound.
A program may use at most 128 MiB of HBM per device.

```python
import math
import jax
import jax.numpy as jnp
from jax import lax

R = 8
W = 64
S = 64
MAXB = 8
VB = 128
NST = 512
POLS = 4
F = 64
FH = 4096
SG = 512
CAP = 16
SLOTS = 128
N_FS = 8


def draw_owners(key, part):
    device_count = 2 * S // CAP
    base_load = CAP // 2
    key_order, key_shift, key_mix = jax.random.split(jax.random.fold_in(key, 11), 3)
    ordering = jax.random.permutation(key_order, device_count)
    shifts = jax.random.randint(key_shift, (device_count // 2,), 0, base_load + 1)
    shifts = shifts.at[0].set(base_load)
    device_loads = jnp.zeros((device_count,), jnp.int32)
    device_loads = device_loads.at[ordering[0::2]].set(base_load + shifts)
    device_loads = device_loads.at[ordering[1::2]].set(base_load - shifts)
    holders = jnp.repeat(jnp.arange(device_count, dtype=jnp.int32), device_loads, total_repeat_length=S)
    return holders[jax.random.permutation(key_mix, S)].astype(jnp.int32)


def draw_counts(key, part):
    key_values, key_place = jax.random.split(jax.random.fold_in(key, 23), 2)
    values = jax.random.randint(key_values, (S,), 1, MAXB + 1)
    position = jax.random.randint(key_place, (), 0, S)
    return values.at[position].set(MAXB).astype(jnp.int32)


def set_ends(entries, stream_key, least, largest):
    longest = entries.shape.index(max(entries.shape))
    spots = []
    for shift in (0, 1):
        where = [jax.random.randint(jax.random.fold_in(stream_key, axis), (), 0, length) for axis, length in enumerate(entries.shape)]
        where[longest] = (where[longest] + shift) % entries.shape[longest]
        spots.append(tuple(where))
    return entries.at[spots[0]].set(least).at[spots[1]].set(largest)


def block_scale(rng, shape, cuts, low, high):
    def one(axis_at, blocks):
        steps = jax.random.uniform(jax.random.fold_in(jax.random.fold_in(rng, 6), axis_at), (blocks,), jnp.float32, low / len(cuts), high / len(cuts))
        return jnp.repeat(jnp.exp(steps), shape[axis_at] // blocks).reshape((-1,) + (1,) * (len(shape) - axis_at - 1))

    gain = one(*cuts[0])
    for cut in cuts[1:]:
        gain = gain * one(*cut)
    return gain


def bell_draw(key, shape, deviation, bound, shards=(), held_as=jnp.bfloat16):
    entries = jax.random.normal(key, shape, jnp.float32) * deviation
    if len(shards) > 0:
        entries = block_scale(key, shape, shards, -0.22, 0.18) * entries
    return jnp.clip(entries, min=-bound, max=bound).astype(held_as)


def setup_inputs(seed: int = 0) -> dict:
    keys = jax.random.split(jax.random.key(seed), 7)
    facets = bell_draw(keys[0], (POLS, F, FH, 2 * W), 1.0, 6.0, ((0, 4), (1, 8)))
    owners = draw_owners(jax.random.fold_in(keys[6], 71), 0)
    counts = draw_counts(jax.random.fold_in(keys[6], 71), 0)
    coords = jnp.clip(512.0 * jax.random.uniform(keys[3], (2, SLOTS, MAXB, VB), jnp.float32) ** block_scale(keys[3], (2, SLOTS, MAXB, VB), ((1, 8),), -0.2, 0.2), 0.0, 512.0)
    station_ids = set_ends(jax.random.randint(keys[4], (SLOTS, MAXB, 2, VB), 0, NST), jax.random.fold_in(keys[4], 1), 0, NST - 1).astype(jnp.int32)
    jones_table = bell_draw(keys[5], (8, NST), 0.5, 3.0, (), jnp.float32)
    return dict(facets=facets, owners=owners, counts=counts, coords=coords, station_ids=station_ids, jones_table=jones_table)


def dft_tables(length):
    indices = jnp.arange(length, dtype=jnp.int32)
    phases = indices[:, None] * indices[None, :] % length
    angles = phases.astype(jnp.float32) * (2.0 * math.pi / length)
    return (jnp.cos(angles).astype(jnp.bfloat16), jnp.sin(angles).astype(jnp.bfloat16))

def turn_table(rows, cols, length):
    row_index = jnp.arange(rows, dtype=jnp.int32)
    col_index = jnp.arange(cols, dtype=jnp.int32)
    phases = row_index[:, None] * col_index[None, :] % length
    angles = phases.astype(jnp.float32) * (2.0 * math.pi / length)
    return (jnp.cos(angles), jnp.sin(angles))

def cell_phases(positions, cells):
    offsets = jnp.arange(cells, dtype=jnp.float32) - cells // 2
    angles = jnp.mod(positions[:, None] * offsets[None, :], float(cells)) * (2.0 * math.pi / cells)
    return (jnp.cos(angles), jnp.sin(angles))

def complex_product(left_real, left_imag, right_real, right_imag):
    return (left_real * right_real - left_imag * right_imag, left_real * right_imag + left_imag * right_real)

def reference(facets, owners, counts, coords, station_ids, jones_table):
    first_cos, first_sin = dft_tables(W)
    second_cos, second_sin = dft_tables(S)
    turn_cos, turn_sin = turn_table(W, S, FH)
    scale = 1.0 / math.sqrt(FH)
    flat_strips = facets.reshape(POLS * F, W, S, 2 * W)

    def transform(strip):
        cos_part = jnp.einsum('kn,nmc->kmc', first_cos, strip, preferred_element_type=jnp.float32)
        sin_part = jnp.einsum('kn,nmc->kmc', first_sin, strip, preferred_element_type=jnp.float32)
        section_real = cos_part[..., :W] + sin_part[..., W:]
        section_imag = cos_part[..., W:] - sin_part[..., :W]
        tc = turn_cos[:, :, None]
        ts = turn_sin[:, :, None]
        turned = jnp.concatenate([section_real * tc + section_imag * ts, section_imag * tc - section_real * ts], axis=2).astype(jnp.bfloat16)
        cos_two = jnp.einsum('qm,kmc->qkc', second_cos, turned, preferred_element_type=jnp.float32)
        sin_two = jnp.einsum('qm,kmc->qkc', second_sin, turned, preferred_element_type=jnp.float32)
        real_part = (cos_two[..., :W] + sin_two[..., W:]) * scale
        imag_part = (cos_two[..., W:] - sin_two[..., :W]) * scale
        return jnp.concatenate([real_part, imag_part], axis=2).reshape(FH, 2 * W).astype(jnp.bfloat16)
    windows = lax.map(transform, flat_strips).reshape(POLS, F, FH, 2 * W)
    owned = (owners[None, :] == jnp.arange(N_FS, dtype=jnp.int32)[:, None]).astype(jnp.int32)
    ranks = jnp.cumsum(owned, axis=1) - 1
    rank_of = lax.optimization_barrier(jnp.sum(owned * ranks, axis=0))
    slot_of = owners * CAP + rank_of

    def predict(index):
        tile = lax.dynamic_slice_in_dim(windows, index * W, W, axis=2)
        real_grid = tile[..., :W].reshape(POLS, R, R, W, W).transpose(0, 1, 3, 2, 4).reshape(POLS, SG, SG)
        imag_grid = tile[..., W:].reshape(POLS, R, R, W, W).transpose(0, 1, 3, 2, 4).reshape(POLS, SG, SG)
        grids = jnp.concatenate([real_grid, imag_grid], axis=2)
        positions = lax.dynamic_index_in_dim(coords, slot_of[index], axis=1, keepdims=False)
        row_cos, row_sin = cell_phases(positions[0].reshape(-1), SG)
        row_cos = row_cos.astype(jnp.bfloat16)
        row_sin = row_sin.astype(jnp.bfloat16)
        col_cos, col_sin = cell_phases(positions[1].reshape(-1), SG)
        results = []
        for pol_index in range(POLS):
            cos_part = jnp.dot(row_cos, grids[pol_index], preferred_element_type=jnp.float32)
            sin_part = jnp.dot(row_sin, grids[pol_index], preferred_element_type=jnp.float32)
            real_part = cos_part[:, :SG] + sin_part[:, SG:]
            imag_part = cos_part[:, SG:] - sin_part[:, :SG]
            vis_real = lax.optimization_barrier(jnp.sum(real_part * col_cos + imag_part * col_sin, axis=1)) / SG
            vis_imag = lax.optimization_barrier(jnp.sum(imag_part * col_cos - real_part * col_sin, axis=1)) / SG
            results.append(jnp.stack([vis_real, vis_imag]).reshape(2, MAXB, VB))
        return jnp.stack(results)
    per_subgrid = lax.map(predict, jnp.arange(S, dtype=jnp.int32))
    matches = owned[:, :, None] * (ranks[:, :, None] == jnp.arange(CAP, dtype=jnp.int32)[None, None, :]).astype(jnp.int32)
    slot_subgrid = lax.optimization_barrier(jnp.sum(matches * jnp.arange(S, dtype=jnp.int32)[None, :, None], axis=1)).reshape(-1)
    slot_valid = lax.optimization_barrier(jnp.sum(matches, axis=1)).reshape(-1)
    visible = jnp.take(per_subgrid, slot_subgrid, axis=0)
    block_limit = jnp.take(counts, slot_subgrid) * slot_valid
    keep = jnp.arange(MAXB, dtype=jnp.int32)[None, :] < block_limit[:, None]
    left = jnp.take(jones_table, station_ids[:, :, 0, :], axis=1)
    right = jnp.take(jones_table, station_ids[:, :, 1, :], axis=1)
    outputs = []
    for row_side in range(2):
        for col_side in range(2):
            total_real = jnp.zeros(visible.shape[:1] + visible.shape[3:], jnp.float32)
            total_imag = jnp.zeros(visible.shape[:1] + visible.shape[3:], jnp.float32)
            for inner_row in range(2):
                for inner_col in range(2):
                    left_entry = 2 * (2 * row_side + inner_row)
                    right_entry = 2 * (2 * col_side + inner_col)
                    comp_real = visible[:, 2 * inner_row + inner_col, 0]
                    comp_imag = visible[:, 2 * inner_row + inner_col, 1]
                    step_real, step_imag = complex_product(left[left_entry], left[left_entry + 1], comp_real, comp_imag)
                    step_real, step_imag = complex_product(step_real, step_imag, right[right_entry], -right[right_entry + 1])
                    total_real = total_real + step_real
                    total_imag = total_imag + step_imag
            outputs.append(jnp.stack([total_real, total_imag]))
    corrected = jnp.stack(outputs)
    return jnp.where(keep[None, None, :, :, None], corrected, 0.0)
```

```python
import functools
import math

import jax
import jax.numpy as jnp
from jax import lax
from jax.experimental import pallas as pl
from jax.experimental.pallas import tpu as pltpu
from jax.sharding import PartitionSpec as P

R = 8
W = 64
S = 64
FH = 4096
SG = 512
UNROLL = 2

SIN_COEFS = [
    (-1) ** i * (2.0 * math.pi) ** (2 * i + 1) / math.factorial(2 * i + 1) for i in range(9)
]
COS_COEFS = [(-1) ** i * (2.0 * math.pi) ** (2 * i) / math.factorial(2 * i) for i in range(10)]


def dft_tables(length):
    indices = jnp.arange(length, dtype=jnp.int32)
    phases = indices[:, None] * indices[None, :] % length
    angles = phases.astype(jnp.float32) * (2.0 * math.pi / length)
    return (jnp.cos(angles).astype(jnp.bfloat16), jnp.sin(angles).astype(jnp.bfloat16))


def turn_table(rows, cols, length):
    row_index = jnp.arange(rows, dtype=jnp.int32)
    col_index = jnp.arange(cols, dtype=jnp.int32)
    phases = row_index[:, None] * col_index[None, :] % length
    angles = phases.astype(jnp.float32) * (2.0 * math.pi / length)
    return (jnp.cos(angles), jnp.sin(angles))


def horner(coefs, square):
    total = jnp.full_like(square, coefs[-1])
    for coef in coefs[-2::-1]:
        total = total * square + coef
    return total


def phase(position, multiple):
    turns = position * (multiple * (1.0 / SG))
    turns = turns - jnp.floor(turns + 0.5)
    square = turns * turns
    return horner(COS_COEFS, square), horner(SIN_COEFS, square) * turns


def twice(left, right):
    return (left[0] * right[0] - left[1] * right[1], left[1] * right[0] + left[0] * right[1])


def predict_kernel(
    facet_local, capacity, index_ref, owners_ref, counts_ref, coords_ref, windows_ref, out_ref,
    items_ref, loads_ref
):
    device_count = out_ref.shape[0]
    max_blocks = out_ref.shape[3]
    uppers = facet_local // 2
    row_start = ((index_ref[0] * facet_local) // R * W - SG // 2).astype(jnp.float32)
    col_start = ((index_ref[0] * facet_local) % R * W - SG // 2).astype(jnp.float32)
    out_ref[...] = jnp.zeros_like(out_ref)

    def clear(i, carry):
        loads_ref[i] = 0
        return carry

    lax.fori_loop(0, device_count, clear, 0)

    def list_items(s, total):
        owner = owners_ref[s]
        load = loads_ref[owner]
        loads_ref[owner] = load + 1
        place = (s * device_count + owner) * capacity + load

        def add(b, t):
            items_ref[t] = place * max_blocks + b
            return t + 1

        return lax.fori_loop(0, counts_ref[s], add, total)

    total = lax.fori_loop(0, owners_ref.shape[0], list_items, 0)

    def pad(i, carry):
        items_ref[total + i] = items_ref[total - 1]
        return carry

    lax.fori_loop(0, UNROLL - 1, pad, 0)
    lane = out_ref.shape[4]
    ramp = lax.broadcasted_iota(jnp.int32, (8, lane), 0).astype(jnp.float32)

    def one(item):
        b = item % max_blocks
        place = item // max_blocks
        load = place % capacity
        owner = (place // capacity) % device_count
        s = place // (capacity * device_count)
        x = coords_ref[owner, 0, load, pl.ds(b, 1), :]
        y = coords_ref[owner, 1, load, pl.ds(b, 1), :]
        fine = phase(y, ramp)
        coarse = [phase(y, ramp * 8.0), phase(y, ramp * 8.0 + 64.0)]
        cos_rows, sin_rows, neg_rows = [], [], []
        for half in coarse:
            c, s_ = half
            cc, ss = twice(
                (c[:, None, :], s_[:, None, :]), (fine[0][None], fine[1][None])
            )
            cos_rows.append(cc.reshape(W, lane).astype(jnp.bfloat16))
            sin_rows.append(ss.reshape(W, lane).astype(jnp.bfloat16))
            neg_rows.append(-sin_rows[-1])
        table = jnp.concatenate(
            [
                jnp.concatenate([cos_rows[0], sin_rows[0], cos_rows[1], sin_rows[1]], axis=0),
                jnp.concatenate([neg_rows[0], cos_rows[0], neg_rows[1], cos_rows[1]], axis=0),
            ],
            axis=1,
        )
        grid = jnp.dot(windows_ref[s], table, preferred_element_type=jnp.float32)
        upper = phase(y, ramp * (2.0 * W) + col_start)
        row_coarse = phase(x, ramp * 8.0 + row_start)
        row_fine = phase(x, ramp)
        sum_real = jnp.zeros((8, lane), jnp.float32)
        sum_imag = jnp.zeros((8, lane), jnp.float32)
        for h in range(uppers):
            mixed = twice((upper[0][h : h + 1], upper[1][h : h + 1]), row_coarse)
            part = grid[h * W : (h + 1) * W].reshape(8, 8, 2 * lane)
            real, imag = part[:, :, :lane], part[:, :, lane:]
            mc, ms = mixed[0][:, None, :], mixed[1][:, None, :]
            sum_real = sum_real + jnp.sum(real * mc + imag * ms, axis=0)
            sum_imag = sum_imag + jnp.sum(imag * mc - real * ms, axis=0)
        fc, fs = row_fine
        vis_real = jnp.sum(sum_real * fc + sum_imag * fs, axis=0, keepdims=True) * (1.0 / SG)
        vis_imag = jnp.sum(sum_imag * fc - sum_real * fs, axis=0, keepdims=True) * (1.0 / SG)
        return owner, load, b, vis_real, vis_imag

    def step(i, carry):
        for owner, load, b, vis_real, vis_imag in [
            one(items_ref[i * UNROLL + u]) for u in range(UNROLL)
        ]:
            out_ref[owner, load, 0, pl.ds(b, 1), :] = vis_real
            out_ref[owner, load, 1, pl.ds(b, 1), :] = vis_imag
        return carry

    lax.fori_loop(0, (total + UNROLL - 1) // UNROLL, step, 0)


def predict(windows, owners, counts, coords, device_index):
    device_count, _, capacity, max_blocks, lane = coords.shape
    facet_local = windows.shape[1] // W * 2
    smem = pl.BlockSpec(memory_space=pltpu.SMEM)
    vmem = pl.BlockSpec(memory_space=pltpu.VMEM)
    return pl.pallas_call(
        functools.partial(predict_kernel, facet_local, capacity),
        out_shape=jax.ShapeDtypeStruct(
            (device_count, capacity, 2, max_blocks, lane), jnp.float32
        ),
        in_specs=[smem, smem, smem, vmem, vmem],
        out_specs=vmem,
        scratch_shapes=[
            pltpu.SMEM((owners.shape[0] * max_blocks + UNROLL,), jnp.int32),
            pltpu.SMEM((device_count,), jnp.int32),
        ],
        compiler_params=pltpu.CompilerParams(vmem_limit_bytes=40 * 2**20),
    )(device_index.reshape(1), owners, counts, coords, windows)


def correct_kernel(index_ref, owners_ref, counts_ref, left_ref, right_ref, table_ref, vis_ref, out_ref):
    capacity = out_ref.shape[1]
    max_blocks, lane = out_ref.shape[2:]
    chunks = table_ref.shape[1] // lane
    me = index_ref[0]
    out_ref[...] = jnp.zeros_like(out_ref)
    block = lax.broadcasted_iota(jnp.int32, (max_blocks, lane), 0)

    def look_up(first, ids):
        low = ids % lane
        high = ids // lane
        found = []
        for row in range(4):
            entry = None
            for chunk in range(chunks):
                source = jnp.broadcast_to(
                    table_ref[first + row : first + row + 1, chunk * lane : (chunk + 1) * lane],
                    (max_blocks, lane),
                )
                got = jnp.take_along_axis(source, low, axis=1, mode="promise_in_bounds")
                entry = got if entry is None else jnp.where(high == chunk, got, entry)
            found.append(entry)
        return [(found[0], found[1]), (found[2], found[3])]

    def product(a, b):
        return (a[0] * b[0] - a[1] * b[1], a[0] * b[1] + a[1] * b[0])

    def slot(s, load):
        is_mine = owners_ref[s] == me

        @pl.when(is_mine)
        def _():
            left = look_up(0, left_ref[load])
            right = look_up(4, right_ref[load])
            total_real = jnp.zeros((max_blocks, lane), jnp.float32)
            total_imag = jnp.zeros((max_blocks, lane), jnp.float32)
            for inner_row in range(2):
                for inner_col in range(2):
                    comp = 2 * inner_row + inner_col
                    step = product(
                        left[inner_row], (vis_ref[comp, load, 0], vis_ref[comp, load, 1])
                    )
                    step = product(step, (right[inner_col][0], -right[inner_col][1]))
                    total_real = total_real + step[0]
                    total_imag = total_imag + step[1]
            keep = block < counts_ref[s]
            out_ref[0, load] = jnp.where(keep, total_real, 0.0)
            out_ref[1, load] = jnp.where(keep, total_imag, 0.0)

        return load + is_mine.astype(jnp.int32)

    lax.fori_loop(0, owners_ref.shape[0], slot, 0)


def correct(visible, owners, counts, station_ids, tables, device_index):
    _, capacity, _, max_blocks, lane = visible.shape
    smem = pl.BlockSpec(memory_space=pltpu.SMEM)
    vmem = pl.BlockSpec(memory_space=pltpu.VMEM)
    return pl.pallas_call(
        correct_kernel,
        out_shape=jax.ShapeDtypeStruct((2, capacity, max_blocks, lane), jnp.float32),
        in_specs=[smem, smem, smem, vmem, vmem, vmem, vmem],
        out_specs=vmem,
    )(
        device_index.reshape(1),
        owners,
        counts,
        station_ids[:, :, 0, :],
        station_ids[:, :, 1, :],
        tables,
        visible,
    )


def transform(strips):
    facet_local = strips.shape[0]
    shaped_strips = strips.reshape(facet_local, W, S, 2 * W)
    first_cos, first_sin = dft_tables(W)
    second_cos, second_sin = dft_tables(S)
    turn_cos, turn_sin = turn_table(W, S, FH)
    scale = 1.0 / math.sqrt(FH)
    cos_part = jnp.einsum(
        "kn,fnmc->fkmc", first_cos, shaped_strips, preferred_element_type=jnp.float32
    )
    sin_part = jnp.einsum(
        "kn,fnmc->fkmc", first_sin, shaped_strips, preferred_element_type=jnp.float32
    )
    section_real = cos_part[..., :W] + sin_part[..., W:]
    section_imag = cos_part[..., W:] - sin_part[..., :W]
    tc = turn_cos[None, :, :, None]
    ts = turn_sin[None, :, :, None]
    turned = jnp.concatenate(
        [section_real * tc + section_imag * ts, section_imag * tc - section_real * ts], axis=3
    ).astype(jnp.bfloat16)
    cos_two = jnp.einsum("qm,fkmc->qfkc", second_cos, turned, preferred_element_type=jnp.float32)
    sin_two = jnp.einsum("qm,fkmc->qfkc", second_sin, turned, preferred_element_type=jnp.float32)
    real_two = (cos_two[..., :W] + sin_two[..., W:]) * scale
    imag_two = (cos_two[..., W:] - sin_two[..., :W]) * scale
    windows = jnp.concatenate([real_two, imag_two], axis=3).astype(jnp.bfloat16)
    windows = windows.reshape(S, facet_local // 2, 2, W, 2 * W)
    return jnp.concatenate([windows[:, :, 0], windows[:, :, 1]], axis=-1).reshape(
        S, facet_local // 2 * W, 4 * W
    )


def on_device(facets, owners, counts, coords, station_ids, jones_table):
    device_index = lax.axis_index("fs").astype(jnp.int32)
    pol_index = lax.axis_index("pol")
    all_coords = lax.all_gather(coords, "fs", axis=0, tiled=False)
    windows = transform(facets[0])
    partial = predict(windows, owners, counts, all_coords, device_index)
    own = lax.psum_scatter(partial, "fs", scatter_dimension=0, tiled=False)
    visible = lax.all_gather(own, "pol", axis=0, tiled=False)
    tables = jnp.concatenate(
        [
            lax.dynamic_slice_in_dim(jones_table, 4 * (pol_index // 2), 4, 0),
            lax.dynamic_slice_in_dim(jones_table, 4 * (pol_index % 2), 4, 0),
        ],
        axis=0,
    )
    return correct(visible, owners, counts, station_ids, tables, device_index)[None]


def solution(mesh):
    return jax.shard_map(
        on_device,
        mesh=mesh,
        in_specs=(
            P("pol", "fs", None, None),
            P(),
            P(),
            P(None, "fs", None, None),
            P("fs", None, None, None),
            P(),
        ),
        out_specs=P("pol", None, "fs", None, None),
        check_vma=False,
    )
```

```python
import functools
import math

import jax
import jax.numpy as jnp
from jax import lax
from jax.experimental import pallas as pl
from jax.experimental.pallas import tpu as pltpu
from jax.sharding import PartitionSpec as P

R = 8
W = 64
S = 64
FH = 4096
SG = 512
UNROLL = 2
GROUP = 2

SIN_COEFS = [
    (-1) ** i * (2.0 * math.pi) ** (2 * i + 1) / math.factorial(2 * i + 1) for i in range(9)
]
COS_COEFS = [(-1) ** i * (2.0 * math.pi) ** (2 * i) / math.factorial(2 * i) for i in range(10)]


def dft_tables(length):
    indices = jnp.arange(length, dtype=jnp.int32)
    phases = indices[:, None] * indices[None, :] % length
    angles = phases.astype(jnp.float32) * (2.0 * math.pi / length)
    return (jnp.cos(angles).astype(jnp.bfloat16), jnp.sin(angles).astype(jnp.bfloat16))


def turn_table(rows, cols, length):
    row_index = jnp.arange(rows, dtype=jnp.int32)
    col_index = jnp.arange(cols, dtype=jnp.int32)
    phases = row_index[:, None] * col_index[None, :] % length
    angles = phases.astype(jnp.float32) * (2.0 * math.pi / length)
    return (jnp.cos(angles), jnp.sin(angles))


def horner(coefs, square):
    total = jnp.full_like(square, coefs[-1])
    for coef in coefs[-2::-1]:
        total = total * square + coef
    return total


def phase(position, multiple):
    turns = position * (multiple * (1.0 / SG))
    turns = turns - jnp.floor(turns + 0.5)
    square = turns * turns
    return horner(COS_COEFS, square), horner(SIN_COEFS, square) * turns


def twice(left, right):
    return (left[0] * right[0] - left[1] * right[1], left[1] * right[0] + left[0] * right[1])


def turn_lanes(values, sign):
    return pltpu.roll(values, W, 1) * sign


def predict_kernel(
    facet_local, capacity, index_ref, owners_ref, counts_ref, coords_ref, first_ref, second_ref,
    turn_cos_ref, turn_sin_ref, strip_ref, out_ref,
    wide_ref, turned_ref, windows_ref, grid_ref, vis_ref, items_ref, loads_ref
):
    facet = pl.program_id(0)
    width = 2 * W
    lanes = lax.broadcasted_iota(jnp.int32, (1, width), 1)
    sign = jnp.where(lanes < W, 1.0, -1.0)

    def widen(i, carry):
        rows = pl.ds(pl.multiple_of(i * 256, 256), 256)
        wide_ref[rows, :] = strip_ref[0, rows, :].astype(jnp.float32)
        return carry

    lax.fori_loop(0, FH // 256, widen, 0)

    def first(i, carry):
        starts = [i * GROUP + u for u in range(GROUP)]
        data = jnp.concatenate(
            [wide_ref[pl.ds(n, W, stride=S), :].astype(jnp.bfloat16) for n in starts], axis=1
        )
        both = jnp.dot(first_ref[...], data, preferred_element_type=jnp.float32)
        for u, n in enumerate(starts):
            part = both[:, u * width : (u + 1) * width]
            rows = pl.ds(pl.multiple_of(n * W, W), W)
            tc, ts = turn_cos_ref[rows, :], turn_sin_ref[rows, :]
            straight = part[:W] * tc - part[W:] * ts
            crossed = part[W:] * tc + part[:W] * ts
            turned_ref[rows, :] = straight + turn_lanes(crossed, sign)
        return carry

    lax.fori_loop(0, S // GROUP, first, 0)

    def second(i, carry):
        starts = [i * GROUP + u for u in range(GROUP)]
        data = jnp.concatenate(
            [turned_ref[pl.ds(k, S, stride=W), :].astype(jnp.bfloat16) for k in starts], axis=1
        )
        both = jnp.dot(second_ref[...], data, preferred_element_type=jnp.float32)
        for u, k in enumerate(starts):
            part = both[:, u * width : (u + 1) * width]
            rows = pl.ds(pl.multiple_of(k * S, S), S)
            windows_ref[facet, rows, :] = part[:S] + turn_lanes(part[S:], sign)
        return carry

    lax.fori_loop(0, W // GROUP, second, 0)

    @pl.when(facet == facet_local - 1)
    def _():
        predict_all(
            facet_local, capacity, index_ref, owners_ref, counts_ref, coords_ref, windows_ref,
            grid_ref, vis_ref, items_ref, loads_ref
        )
        out_ref[...] = vis_ref[...].astype(jnp.bfloat16)


def predict_all(
    facet_local, capacity, index_ref, owners_ref, counts_ref, coords_ref, windows_ref,
    grid_ref, out_ref, items_ref, loads_ref
):
    device_count = out_ref.shape[0]
    max_blocks = out_ref.shape[3]
    uppers = facet_local // 2
    scale = 1.0 / (math.sqrt(FH) * SG)
    row_start = ((index_ref[0] * facet_local) // R * W - SG // 2).astype(jnp.float32)
    col_start = ((index_ref[0] * facet_local) % R * W - SG // 2).astype(jnp.float32)
    out_ref[...] = jnp.zeros_like(out_ref)

    def clear(i, carry):
        loads_ref[i] = 0
        return carry

    lax.fori_loop(0, device_count, clear, 0)

    def list_items(s, total):
        owner = owners_ref[s]
        load = loads_ref[owner]
        loads_ref[owner] = load + 1
        place = (s * device_count + owner) * capacity + load

        def add(b, t):
            items_ref[t] = place * max_blocks + b
            return t + 1

        return lax.fori_loop(0, counts_ref[s], add, total)

    total = lax.fori_loop(0, owners_ref.shape[0], list_items, 0)

    def pad(i, carry):
        items_ref[total + i] = items_ref[total - 1]
        return carry

    lax.fori_loop(0, UNROLL - 1, pad, 0)
    lane = out_ref.shape[4]
    ramp = lax.broadcasted_iota(jnp.int32, (8, lane), 0).astype(jnp.float32)

    def pack(s, carry):
        for f in range(facet_local):
            rows = slice(f // 2 * W, (f // 2 + 1) * W)
            cols = slice(f % 2 * 2 * W, (f % 2 + 1) * 2 * W)
            grid_ref[s, rows, cols] = windows_ref[f, pl.ds(s, W, stride=S), :].astype(
                jnp.bfloat16
            )
        return carry

    lax.fori_loop(0, S, pack, 0)

    def one(item):
        b = item % max_blocks
        place = item // max_blocks
        load = place % capacity
        owner = (place // capacity) % device_count
        s = place // (capacity * device_count)
        x = coords_ref[owner, 0, load, pl.ds(b, 1), :]
        y = coords_ref[owner, 1, load, pl.ds(b, 1), :]
        fine = phase(y, ramp)
        coarse = [phase(y, ramp * 8.0), phase(y, ramp * 8.0 + 64.0)]
        cos_rows, sin_rows, neg_rows = [], [], []
        for half in coarse:
            c, s_ = half
            cc, ss = twice(
                (c[:, None, :], s_[:, None, :]), (fine[0][None], fine[1][None])
            )
            cos_rows.append(cc.reshape(W, lane).astype(jnp.bfloat16))
            sin_rows.append(ss.reshape(W, lane).astype(jnp.bfloat16))
            neg_rows.append(-sin_rows[-1])
        table = jnp.concatenate(
            [
                jnp.concatenate([cos_rows[0], sin_rows[0], cos_rows[1], sin_rows[1]], axis=0),
                jnp.concatenate([neg_rows[0], cos_rows[0], neg_rows[1], cos_rows[1]], axis=0),
            ],
            axis=1,
        )
        grid = jnp.dot(grid_ref[s], table, preferred_element_type=jnp.float32)
        upper = phase(y, ramp * (2.0 * W) + col_start)
        row_coarse = phase(x, ramp * 8.0 + row_start)
        row_fine = phase(x, ramp)
        sum_real = jnp.zeros((8, lane), jnp.float32)
        sum_imag = jnp.zeros((8, lane), jnp.float32)
        for h in range(uppers):
            mixed = twice((upper[0][h : h + 1], upper[1][h : h + 1]), row_coarse)
            part = grid[h * W : (h + 1) * W].reshape(8, 8, 2 * lane)
            real, imag = part[:, :, :lane], part[:, :, lane:]
            mc, ms = mixed[0][:, None, :], mixed[1][:, None, :]
            sum_real = sum_real + jnp.sum(real * mc + imag * ms, axis=0)
            sum_imag = sum_imag + jnp.sum(imag * mc - real * ms, axis=0)
        fc, fs = row_fine
        vis_real = jnp.sum(sum_real * fc + sum_imag * fs, axis=0, keepdims=True) * scale
        vis_imag = jnp.sum(sum_imag * fc - sum_real * fs, axis=0, keepdims=True) * scale
        return owner, load, b, vis_real, vis_imag

    def step(i, carry):
        for owner, load, b, vis_real, vis_imag in [
            one(items_ref[i * UNROLL + u]) for u in range(UNROLL)
        ]:
            out_ref[owner, load, 0, pl.ds(b, 1), :] = vis_real
            out_ref[owner, load, 1, pl.ds(b, 1), :] = vis_imag
        return carry

    lax.fori_loop(0, (total + UNROLL - 1) // UNROLL, step, 0)


def predict(strips, owners, counts, coords, device_index):
    device_count, _, capacity, max_blocks, lane = coords.shape
    facet_local = strips.shape[0]
    smem = pl.BlockSpec(memory_space=pltpu.SMEM)
    whole = lambda *shape: pl.BlockSpec(shape, lambda f: (0,) * len(shape))
    first = jnp.concatenate(dft_tables(W), axis=0)
    second = jnp.concatenate(dft_tables(S), axis=0)
    turns = [
        jnp.broadcast_to(table.T[:, :, None], (S, W, 2 * W)).reshape(FH, 2 * W)
        for table in turn_table(W, S, FH)
    ]
    slots = (device_count, capacity, 2, max_blocks, lane)
    return pl.pallas_call(
        functools.partial(predict_kernel, facet_local, capacity),
        out_shape=jax.ShapeDtypeStruct(slots, jnp.bfloat16),
        grid=(facet_local,),
        in_specs=[
            smem, smem, smem,
            whole(*coords.shape),
            whole(2 * W, W),
            whole(2 * S, S),
            whole(FH, 2 * W),
            whole(FH, 2 * W),
            pl.BlockSpec((1, FH, 2 * W), lambda f: (f, 0, 0)),
        ],
        out_specs=whole(*slots),
        scratch_shapes=[
            pltpu.VMEM((FH, 2 * W), jnp.float32),
            pltpu.VMEM((FH, 2 * W), jnp.float32),
            pltpu.VMEM((facet_local, FH, 2 * W), jnp.float32),
            pltpu.VMEM((S, facet_local // 2 * W, 4 * W), jnp.bfloat16),
            pltpu.VMEM(slots, jnp.float32),
            pltpu.SMEM((owners.shape[0] * max_blocks + UNROLL,), jnp.int32),
            pltpu.SMEM((device_count,), jnp.int32),
        ],
        compiler_params=pltpu.CompilerParams(vmem_limit_bytes=58 * 2**20),
    )(device_index.reshape(1), owners, counts, coords, first, second, *turns, strips)


def add_up_kernel(device_count, in_ref, out_ref, arrived_ref, send_sem, recv_sem):
    me = lax.axis_index("fs")
    barrier = pltpu.get_barrier_semaphore()
    peers = [lax.rem(me + step, device_count) for step in range(1, device_count)]
    for peer in peers:
        pl.semaphore_signal(
            barrier, inc=1, device_id={"fs": peer}, device_id_type=pl.DeviceIdType.MESH
        )
    pl.semaphore_wait(barrier, device_count - 1)
    copies = []
    for i, peer in enumerate(peers):
        copy = pltpu.make_async_remote_copy(
            src_ref=in_ref.at[peer],
            dst_ref=arrived_ref.at[i],
            send_sem=send_sem.at[i],
            recv_sem=recv_sem.at[i],
            device_id={"fs": peer},
            device_id_type=pl.DeviceIdType.MESH,
        )
        copy.start()
        copies.append(copy)
    out_ref[...] = in_ref[me].astype(jnp.float32)
    for i, copy in enumerate(copies):
        copy.wait_recv()
        out_ref[...] += arrived_ref[i].astype(jnp.float32)
    for copy in copies:
        copy.wait_send()


def add_up(parts):
    device_count = parts.shape[0]
    vmem = pl.BlockSpec(memory_space=pltpu.VMEM)
    return pl.pallas_call(
        functools.partial(add_up_kernel, device_count),
        out_shape=jax.ShapeDtypeStruct(parts.shape[1:], jnp.float32),
        in_specs=[vmem],
        out_specs=vmem,
        scratch_shapes=[
            pltpu.VMEM((device_count - 1,) + parts.shape[1:], jnp.bfloat16),
            pltpu.SemaphoreType.DMA((device_count - 1,)),
            pltpu.SemaphoreType.DMA((device_count - 1,)),
        ],
        compiler_params=pltpu.CompilerParams(collective_id=0, has_side_effects=True),
    )(parts)


def correct_kernel(index_ref, owners_ref, counts_ref, left_ref, right_ref, table_ref, vis_ref, out_ref):
    capacity = out_ref.shape[1]
    max_blocks, lane = out_ref.shape[2:]
    chunks = table_ref.shape[1] // lane
    me = index_ref[0]
    out_ref[...] = jnp.zeros_like(out_ref)
    block = lax.broadcasted_iota(jnp.int32, (max_blocks, lane), 0)

    def look_up(first, ids):
        low = ids % lane
        high = ids // lane
        found = []
        for row in range(4):
            entry = None
            for chunk in range(chunks):
                source = jnp.broadcast_to(
                    table_ref[first + row : first + row + 1, chunk * lane : (chunk + 1) * lane],
                    (max_blocks, lane),
                )
                got = jnp.take_along_axis(source, low, axis=1, mode="promise_in_bounds")
                entry = got if entry is None else jnp.where(high == chunk, got, entry)
            found.append(entry)
        return [(found[0], found[1]), (found[2], found[3])]

    def product(a, b):
        return (a[0] * b[0] - a[1] * b[1], a[0] * b[1] + a[1] * b[0])

    def slot(s, load):
        is_mine = owners_ref[s] == me

        @pl.when(is_mine)
        def _():
            left = look_up(0, left_ref[load])
            right = look_up(4, right_ref[load])
            total_real = jnp.zeros((max_blocks, lane), jnp.float32)
            total_imag = jnp.zeros((max_blocks, lane), jnp.float32)
            for inner_row in range(2):
                for inner_col in range(2):
                    comp = 2 * inner_row + inner_col
                    step = product(
                        left[inner_row], (vis_ref[comp, load, 0], vis_ref[comp, load, 1])
                    )
                    step = product(step, (right[inner_col][0], -right[inner_col][1]))
                    total_real = total_real + step[0]
                    total_imag = total_imag + step[1]
            keep = block < counts_ref[s]
            out_ref[0, load] = jnp.where(keep, total_real, 0.0)
            out_ref[1, load] = jnp.where(keep, total_imag, 0.0)

        return load + is_mine.astype(jnp.int32)

    lax.fori_loop(0, owners_ref.shape[0], slot, 0)


def correct(visible, owners, counts, station_ids, tables, device_index):
    _, capacity, _, max_blocks, lane = visible.shape
    smem = pl.BlockSpec(memory_space=pltpu.SMEM)
    vmem = pl.BlockSpec(memory_space=pltpu.VMEM)
    return pl.pallas_call(
        correct_kernel,
        out_shape=jax.ShapeDtypeStruct((2, capacity, max_blocks, lane), jnp.float32),
        in_specs=[smem, smem, smem, vmem, vmem, vmem, vmem],
        out_specs=vmem,
    )(
        device_index.reshape(1),
        owners,
        counts,
        station_ids[:, :, 0, :],
        station_ids[:, :, 1, :],
        tables,
        visible,
    )


def on_device(facets, owners, counts, coords, station_ids, jones_table):
    device_index = lax.axis_index("fs").astype(jnp.int32)
    pol_index = lax.axis_index("pol")
    all_coords = lax.all_gather(coords, "fs", axis=0, tiled=False)
    own = add_up(predict(facets[0], owners, counts, all_coords, device_index))
    visible = lax.all_gather(own, "pol", axis=0, tiled=False)
    tables = jnp.concatenate(
        [
            lax.dynamic_slice_in_dim(jones_table, 4 * (pol_index // 2), 4, 0),
            lax.dynamic_slice_in_dim(jones_table, 4 * (pol_index % 2), 4, 0),
        ],
        axis=0,
    )
    return correct(visible, owners, counts, station_ids, tables, device_index)[None]


def solution(mesh):
    return jax.shard_map(
        on_device,
        mesh=mesh,
        in_specs=(
            P("pol", "fs", None, None),
            P(),
            P(),
            P(None, "fs", None, None),
            P("fs", None, None, None),
            P(),
        ),
        out_specs=P("pol", None, "fs", None, None),
        check_vma=False,
    )
```

```python
import functools
import math

import jax
import jax.numpy as jnp
from jax import lax
from jax.experimental import pallas as pl
from jax.experimental.pallas import tpu as pltpu
from jax.sharding import PartitionSpec as P

R = 8
W = 64
S = 64
FH = 4096
SG = 512
UNROLL = 4
GROUP = 4

SIN_COEFS = [
    (-1) ** i * math.pi ** (2 * i + 1) / math.factorial(2 * i + 1) for i in range(6)
]
COS_COEFS = [(-1) ** i * math.pi ** (2 * i) / math.factorial(2 * i) for i in range(7)]


def dft_tables(length):
    indices = jnp.arange(length, dtype=jnp.int32)
    phases = indices[:, None] * indices[None, :] % length
    angles = phases.astype(jnp.float32) * (2.0 * math.pi / length)
    return (jnp.cos(angles).astype(jnp.bfloat16), jnp.sin(angles).astype(jnp.bfloat16))


def turn_table(rows, cols, length):
    row_index = jnp.arange(rows, dtype=jnp.int32)
    col_index = jnp.arange(cols, dtype=jnp.int32)
    phases = row_index[:, None] * col_index[None, :] % length
    angles = phases.astype(jnp.float32) * (2.0 * math.pi / length)
    return (jnp.cos(angles), jnp.sin(angles))


def horner(coefs, square):
    total = jnp.full_like(square, coefs[-1])
    for coef in coefs[-2::-1]:
        total = total * square + coef
    return total


def phase(position, multiple):
    halves = position * (multiple * (2.0 / SG))
    nearest = jnp.floor(halves + 0.5)
    rest = halves - nearest
    square = rest * rest
    pairs = nearest * 0.5
    flip = 1.0 - 4.0 * (pairs - jnp.floor(pairs))
    return horner(COS_COEFS, square) * flip, horner(SIN_COEFS, square) * (rest * flip)


def twice(left, right):
    return (left[0] * right[0] - left[1] * right[1], left[1] * right[0] + left[0] * right[1])


def turn_lanes(values, sign):
    return pltpu.roll(values, W, 1) * sign


def transform_kernel(
    first_ref, second_ref, turn_cos_ref, turn_sin_ref, strip_ref, out_ref, turned_ref, window_ref
):
    width = 2 * W
    lanes = lax.broadcasted_iota(jnp.int32, (1, width), 1)
    sign = jnp.where(lanes < W, 1.0, -1.0)

    def first(i, carry):
        start = pl.multiple_of(i * 16, 16)
        strips = jnp.swapaxes(strip_ref[0, :, pl.ds(start, 16), :].astype(jnp.float32), 0, 1)
        strips = strips.astype(jnp.bfloat16)
        for j in range(0, 16, GROUP):
            data = jnp.concatenate([strips[j + u] for u in range(GROUP)], axis=1)
            both = jnp.dot(first_ref[...], data, preferred_element_type=jnp.float32)
            for u in range(GROUP):
                n = start + j + u
                part = both[:, u * width : (u + 1) * width]
                tc, ts = turn_cos_ref[n], turn_sin_ref[n]
                straight = part[:W] * tc - part[W:] * ts
                crossed = part[W:] * tc + part[:W] * ts
                turned_ref[n] = straight + turn_lanes(crossed, sign)
        return carry

    lax.fori_loop(0, S // 16, first, 0)

    def second(i, carry):
        start = pl.multiple_of(i * 8, 8)
        turned = jnp.swapaxes(turned_ref[:, pl.ds(start, 8), :], 0, 1).astype(jnp.bfloat16)
        for j in range(0, 8, GROUP):
            data = jnp.concatenate([turned[j + u] for u in range(GROUP)], axis=1)
            both = jnp.dot(second_ref[...], data, preferred_element_type=jnp.float32)
            for u in range(GROUP):
                part = both[:, u * width : (u + 1) * width]
                window_ref[start + j + u] = part[:S] + turn_lanes(part[S:], sign)
        return carry

    lax.fori_loop(0, W // 8, second, 0)

    def third(i, carry):
        start = pl.multiple_of(i * 8, 8)
        windows = jnp.swapaxes(window_ref[:, pl.ds(start, 8), :], 0, 1)
        out_ref[pl.ds(start, 8), 0] = windows.astype(jnp.bfloat16)
        return carry

    lax.fori_loop(0, S // 8, third, 0)


def turn_lanes(values, sign):
    return pltpu.roll(values, W, 1) * sign


def transform(strips):
    facet_local = strips.shape[0]
    whole = lambda *shape: pl.BlockSpec(shape, lambda f: (0,) * len(shape))
    turns = [
        jnp.broadcast_to(table.T[:, :, None], (S, W, 2 * W)) for table in turn_table(W, S, FH)
    ]
    windows = pl.pallas_call(
        transform_kernel,
        out_shape=jax.ShapeDtypeStruct((S, facet_local // 2, W, 4 * W), jnp.bfloat16),
        grid=(facet_local,),
        in_specs=[
            whole(2 * W, W),
            whole(2 * S, S),
            whole(S, W, 2 * W),
            whole(S, W, 2 * W),
            pl.BlockSpec((1, W, S, 2 * W), lambda f: (f, 0, 0, 0)),
        ],
        out_specs=pl.BlockSpec((S, 1, W, 2 * W), lambda f: (0, f // 2, 0, f % 2)),
        scratch_shapes=[
            pltpu.VMEM((S, W, 2 * W), jnp.float32),
            pltpu.VMEM((W, S, 2 * W), jnp.float32),
        ],
        compiler_params=pltpu.CompilerParams(vmem_limit_bytes=32 * 2**20),
        cost_estimate=pl.CostEstimate(
            flops=5 * 10**10, bytes_accessed=64 * 2**20, transcendentals=0
        ),
    )(
        jnp.concatenate(dft_tables(W), axis=0),
        jnp.concatenate(dft_tables(S), axis=0),
        *turns,
        strips.reshape(facet_local, W, S, 2 * W),
    )
    return windows.reshape(S, facet_local // 2 * W, 4 * W)


def predict_kernel(
    facet_local, capacity, index_ref, owners_ref, counts_ref, coords_ref, windows_ref, parts_ref,
    out_ref, items_ref, loads_ref
):
    device_count = out_ref.shape[0]
    max_blocks = out_ref.shape[3]
    uppers = facet_local // 2
    scale = 1.0 / (math.sqrt(FH) * SG)
    row_start = ((index_ref[0] * facet_local) // R * W - SG // 2).astype(jnp.float32)
    col_start = ((index_ref[0] * facet_local) % R * W - SG // 2).astype(jnp.float32)
    out_ref[...] = jnp.zeros_like(out_ref)

    def clear(i, carry):
        loads_ref[i] = 0
        return carry

    lax.fori_loop(0, device_count, clear, 0)

    def list_items(s, total):
        owner = owners_ref[s]
        load = loads_ref[owner]
        loads_ref[owner] = load + 1
        place = (s * device_count + owner) * capacity + load

        def add(b, t):
            items_ref[t] = place * max_blocks + b
            return t + 1

        return lax.fori_loop(0, counts_ref[s], add, total)

    total = lax.fori_loop(0, owners_ref.shape[0], list_items, 0)

    def pad(i, carry):
        items_ref[total + i] = items_ref[total - 1]
        return carry

    lax.fori_loop(0, UNROLL - 1, pad, 0)
    lane = out_ref.shape[4]
    ramp = lax.broadcasted_iota(jnp.int32, (8, lane), 0).astype(jnp.float32)

    def one(item):
        b = item % max_blocks
        place = item // max_blocks
        load = place % capacity
        owner = (place // capacity) % device_count
        s = place // (capacity * device_count)
        x = coords_ref[owner, 0, load, pl.ds(b, 1), :]
        y = coords_ref[owner, 1, load, pl.ds(b, 1), :]
        fine = phase(y, ramp)
        upper = phase(y, jnp.where(ramp < uppers, ramp * (2.0 * W) + col_start, 1.0 * W))
        coarse = phase(y, ramp * 8.0)
        coarse = [coarse, twice(coarse, (upper[0][uppers:uppers + 1], upper[1][uppers:uppers + 1]))]
        cos_rows, sin_rows, neg_rows = [], [], []
        for half in coarse:
            c, s_ = half
            cc, ss = twice(
                (c[:, None, :], s_[:, None, :]), (fine[0][None], fine[1][None])
            )
            cos_rows.append(cc.reshape(W, lane).astype(jnp.bfloat16))
            sin_rows.append(ss.reshape(W, lane).astype(jnp.bfloat16))
            neg_rows.append(-sin_rows[-1])
        table = jnp.concatenate(
            [
                jnp.concatenate([cos_rows[0], sin_rows[0], cos_rows[1], sin_rows[1]], axis=0),
                jnp.concatenate([neg_rows[0], cos_rows[0], neg_rows[1], cos_rows[1]], axis=0),
            ],
            axis=1,
        )
        grid = jnp.dot(windows_ref[s], table, preferred_element_type=jnp.float32)
        row_coarse = phase(x, ramp * 8.0 + row_start)
        row_fine = phase(x, ramp)
        sum_real = jnp.zeros((8, lane), jnp.float32)
        sum_imag = jnp.zeros((8, lane), jnp.float32)
        for h in range(uppers):
            mixed = twice((upper[0][h : h + 1], upper[1][h : h + 1]), row_coarse)
            part = grid[h * W : (h + 1) * W].reshape(8, 8, 2 * lane)
            real, imag = part[:, :, :lane], part[:, :, lane:]
            mc, ms = mixed[0][:, None, :], mixed[1][:, None, :]
            sum_real = sum_real + jnp.sum(real * mc + imag * ms, axis=0)
            sum_imag = sum_imag + jnp.sum(imag * mc - real * ms, axis=0)
        fc, fs = row_fine
        vis_real = jnp.sum(sum_real * fc + sum_imag * fs, axis=0, keepdims=True) * scale
        vis_imag = jnp.sum(sum_imag * fc - sum_real * fs, axis=0, keepdims=True) * scale
        return owner, load, b, vis_real, vis_imag

    def step(i, carry):
        for owner, load, b, vis_real, vis_imag in [
            one(items_ref[i * UNROLL + u]) for u in range(UNROLL)
        ]:
            out_ref[owner, load, 0, pl.ds(b, 1), :] = vis_real
            out_ref[owner, load, 1, pl.ds(b, 1), :] = vis_imag
        return carry

    lax.fori_loop(0, (total + UNROLL - 1) // UNROLL, step, 0)
    parts_ref[...] = out_ref[...].astype(jnp.bfloat16)


def predict(windows, owners, counts, coords, device_index):
    device_count, _, capacity, max_blocks, lane = coords.shape
    facet_local = windows.shape[1] // W * 2
    smem = pl.BlockSpec(memory_space=pltpu.SMEM)
    vmem = pl.BlockSpec(memory_space=pltpu.VMEM)
    slots = (device_count, capacity, 2, max_blocks, lane)
    return pl.pallas_call(
        functools.partial(predict_kernel, facet_local, capacity),
        out_shape=jax.ShapeDtypeStruct(slots, jnp.bfloat16),
        in_specs=[smem, smem, smem, vmem, vmem],
        out_specs=vmem,
        scratch_shapes=[
            pltpu.VMEM(slots, jnp.float32),
            pltpu.SMEM((owners.shape[0] * max_blocks + UNROLL,), jnp.int32),
            pltpu.SMEM((device_count,), jnp.int32),
        ],
        compiler_params=pltpu.CompilerParams(vmem_limit_bytes=40 * 2**20),
    )(device_index.reshape(1), owners, counts, coords, windows)


def add_up_kernel(device_count, in_ref, out_ref, arrived_ref, send_sem, recv_sem):
    me = lax.axis_index("fs")
    barrier = pltpu.get_barrier_semaphore()
    peers = [lax.rem(me + step, device_count) for step in range(1, device_count)]
    for peer in peers:
        pl.semaphore_signal(
            barrier, inc=1, device_id={"fs": peer}, device_id_type=pl.DeviceIdType.MESH
        )
    pl.semaphore_wait(barrier, device_count - 1)
    copies = []
    for i, peer in enumerate(peers):
        copy = pltpu.make_async_remote_copy(
            src_ref=in_ref.at[peer],
            dst_ref=arrived_ref.at[i],
            send_sem=send_sem.at[i],
            recv_sem=recv_sem.at[i],
            device_id={"fs": peer},
            device_id_type=pl.DeviceIdType.MESH,
        )
        copy.start()
        copies.append(copy)
    out_ref[...] = in_ref[me].astype(jnp.float32)
    for i, copy in enumerate(copies):
        copy.wait_recv()
        out_ref[...] += arrived_ref[i].astype(jnp.float32)
    for copy in copies:
        copy.wait_send()


def add_up(parts):
    device_count = parts.shape[0]
    vmem = pl.BlockSpec(memory_space=pltpu.VMEM)
    return pl.pallas_call(
        functools.partial(add_up_kernel, device_count),
        out_shape=jax.ShapeDtypeStruct(parts.shape[1:], jnp.float32),
        in_specs=[vmem],
        out_specs=vmem,
        scratch_shapes=[
            pltpu.VMEM((device_count - 1,) + parts.shape[1:], jnp.bfloat16),
            pltpu.SemaphoreType.DMA((device_count - 1,)),
            pltpu.SemaphoreType.DMA((device_count - 1,)),
        ],
        compiler_params=pltpu.CompilerParams(collective_id=0, has_side_effects=True),
    )(parts)


def correct_kernel(index_ref, owners_ref, counts_ref, left_ref, right_ref, table_ref, vis_ref, out_ref):
    capacity = out_ref.shape[1]
    max_blocks, lane = out_ref.shape[2:]
    chunks = table_ref.shape[1] // lane
    me = index_ref[0]
    out_ref[...] = jnp.zeros_like(out_ref)
    block = lax.broadcasted_iota(jnp.int32, (max_blocks, lane), 0)

    def look_up(first, ids):
        low = ids % lane
        high = ids // lane
        found = []
        for row in range(4):
            entry = None
            for chunk in range(chunks):
                source = jnp.broadcast_to(
                    table_ref[first + row : first + row + 1, chunk * lane : (chunk + 1) * lane],
                    (max_blocks, lane),
                )
                got = jnp.take_along_axis(source, low, axis=1, mode="promise_in_bounds")
                entry = got if entry is None else jnp.where(high == chunk, got, entry)
            found.append(entry)
        return [(found[0], found[1]), (found[2], found[3])]

    def product(a, b):
        return (a[0] * b[0] - a[1] * b[1], a[0] * b[1] + a[1] * b[0])

    def slot(s, load):
        is_mine = owners_ref[s] == me

        @pl.when(is_mine)
        def _():
            left = look_up(0, left_ref[load])
            right = look_up(4, right_ref[load])
            total_real = jnp.zeros((max_blocks, lane), jnp.float32)
            total_imag = jnp.zeros((max_blocks, lane), jnp.float32)
            for inner_row in range(2):
                for inner_col in range(2):
                    comp = 2 * inner_row + inner_col
                    step = product(
                        left[inner_row], (vis_ref[comp, load, 0], vis_ref[comp, load, 1])
                    )
                    step = product(step, (right[inner_col][0], -right[inner_col][1]))
                    total_real = total_real + step[0]
                    total_imag = total_imag + step[1]
            keep = block < counts_ref[s]
            out_ref[0, load] = jnp.where(keep, total_real, 0.0)
            out_ref[1, load] = jnp.where(keep, total_imag, 0.0)

        return load + is_mine.astype(jnp.int32)

    lax.fori_loop(0, owners_ref.shape[0], slot, 0)


def correct(visible, owners, counts, station_ids, tables, device_index):
    _, capacity, _, max_blocks, lane = visible.shape
    smem = pl.BlockSpec(memory_space=pltpu.SMEM)
    vmem = pl.BlockSpec(memory_space=pltpu.VMEM)
    return pl.pallas_call(
        correct_kernel,
        out_shape=jax.ShapeDtypeStruct((2, capacity, max_blocks, lane), jnp.float32),
        in_specs=[smem, smem, smem, vmem, vmem, vmem, vmem],
        out_specs=vmem,
    )(
        device_index.reshape(1),
        owners,
        counts,
        station_ids[:, :, 0, :],
        station_ids[:, :, 1, :],
        tables,
        visible,
    )


def on_device(facets, owners, counts, coords, station_ids, jones_table):
    device_index = lax.axis_index("fs").astype(jnp.int32)
    pol_index = lax.axis_index("pol")
    all_coords = lax.all_gather(coords, "fs", axis=0, tiled=False)
    own = add_up(predict(transform(facets[0]), owners, counts, all_coords, device_index))
    visible = lax.all_gather(own, "pol", axis=0, tiled=False)
    tables = jnp.concatenate(
        [
            lax.dynamic_slice_in_dim(jones_table, 4 * (pol_index // 2), 4, 0),
            lax.dynamic_slice_in_dim(jones_table, 4 * (pol_index % 2), 4, 0),
        ],
        axis=0,
    )
    return correct(visible, owners, counts, station_ids, tables, device_index)[None]


def solution(mesh):
    return jax.shard_map(
        on_device,
        mesh=mesh,
        in_specs=(
            P("pol", "fs", None, None),
            P(),
            P(),
            P(None, "fs", None, None),
            P("fs", None, None, None),
            P(),
        ),
        out_specs=P("pol", None, "fs", None, None),
        check_vma=False,
    )
```

```python
import functools
import math

import jax
import jax.numpy as jnp
from jax import lax
from jax.experimental import pallas as pl
from jax.experimental.pallas import tpu as pltpu
from jax.sharding import PartitionSpec as P

R = 8
W = 64
S = 64
FH = 4096
SG = 512
UNROLL = 4
GROUP = 4

SIN_COEFS = [
    (-1) ** i * math.pi ** (2 * i + 1) / math.factorial(2 * i + 1) for i in range(6)
]
COS_COEFS = [(-1) ** i * math.pi ** (2 * i) / math.factorial(2 * i) for i in range(7)]


def dft_tables(length):
    indices = jnp.arange(length, dtype=jnp.int32)
    phases = indices[:, None] * indices[None, :] % length
    angles = phases.astype(jnp.float32) * (2.0 * math.pi / length)
    return (jnp.cos(angles).astype(jnp.bfloat16), jnp.sin(angles).astype(jnp.bfloat16))


def turn_table(rows, cols, length):
    row_index = jnp.arange(rows, dtype=jnp.int32)
    col_index = jnp.arange(cols, dtype=jnp.int32)
    phases = row_index[:, None] * col_index[None, :] % length
    angles = phases.astype(jnp.float32) * (2.0 * math.pi / length)
    return (jnp.cos(angles), jnp.sin(angles))


def horner(coefs, square):
    total = jnp.full_like(square, coefs[-1])
    for coef in coefs[-2::-1]:
        total = total * square + coef
    return total


def phase(position, multiple):
    halves = position * (multiple * (2.0 / SG))
    nearest = jnp.floor(halves + 0.5)
    rest = halves - nearest
    square = rest * rest
    pairs = nearest * 0.5
    flip = 1.0 - 4.0 * (pairs - jnp.floor(pairs))
    return horner(COS_COEFS, square) * flip, horner(SIN_COEFS, square) * (rest * flip)


def twice(left, right):
    return (left[0] * right[0] - left[1] * right[1], left[1] * right[0] + left[0] * right[1])


def turn_lanes(values, sign):
    return pltpu.roll(values, W, 1) * sign


def transform_kernel(
    device_count, first_ref, second_ref, turn_cos_ref, turn_sin_ref, coords_ref, strip_ref, out_ref,
    gathered_ref, turned_ref, window_ref, everyone_ref, own_sem, send_sem, recv_sem
):
    me = lax.axis_index("fs")
    copies = [
        pltpu.make_async_remote_copy(
            src_ref=everyone_ref.at[me],
            dst_ref=everyone_ref.at[me],
            send_sem=send_sem.at[step],
            recv_sem=recv_sem.at[step],
            device_id={"fs": lax.rem(me + step + 1, device_count)},
            device_id_type=pl.DeviceIdType.MESH,
        )
        for step in range(device_count - 1)
    ]

    @pl.when(pl.program_id(0) == 0)
    def _():
        own = pltpu.make_async_copy(coords_ref, everyone_ref.at[me], own_sem)
        own.start()
        barrier = pltpu.get_barrier_semaphore()
        for step in range(device_count - 1):
            pl.semaphore_signal(
                barrier,
                inc=1,
                device_id={"fs": lax.rem(me + step + 1, device_count)},
                device_id_type=pl.DeviceIdType.MESH,
            )
        pl.semaphore_wait(barrier, device_count - 1)
        own.wait()
        for copy in copies:
            copy.start()

    width = 2 * W
    lanes = lax.broadcasted_iota(jnp.int32, (1, width), 1)
    sign = jnp.where(lanes < W, 1.0, -1.0)

    def first(i, carry):
        start = pl.multiple_of(i * 16, 16)
        strips = jnp.swapaxes(strip_ref[0, :, pl.ds(start, 16), :].astype(jnp.float32), 0, 1)
        strips = strips.astype(jnp.bfloat16)
        for j in range(0, 16, GROUP):
            data = jnp.concatenate([strips[j + u] for u in range(GROUP)], axis=1)
            both = jnp.dot(first_ref[...], data, preferred_element_type=jnp.float32)
            for u in range(GROUP):
                n = start + j + u
                part = both[:, u * width : (u + 1) * width]
                tc, ts = turn_cos_ref[n], turn_sin_ref[n]
                straight = part[:W] * tc - part[W:] * ts
                crossed = part[W:] * tc + part[:W] * ts
                turned_ref[n] = straight + turn_lanes(crossed, sign)
        return carry

    lax.fori_loop(0, S // 16, first, 0)

    def second(i, carry):
        start = pl.multiple_of(i * 8, 8)
        turned = jnp.swapaxes(turned_ref[:, pl.ds(start, 8), :], 0, 1).astype(jnp.bfloat16)
        for j in range(0, 8, GROUP):
            data = jnp.concatenate([turned[j + u] for u in range(GROUP)], axis=1)
            both = jnp.dot(second_ref[...], data, preferred_element_type=jnp.float32)
            for u in range(GROUP):
                part = both[:, u * width : (u + 1) * width]
                window_ref[start + j + u] = part[:S] + turn_lanes(part[S:], sign)
        return carry

    lax.fori_loop(0, W // 8, second, 0)

    def third(i, carry):
        start = pl.multiple_of(i * 8, 8)
        windows = jnp.swapaxes(window_ref[:, pl.ds(start, 8), :], 0, 1)
        out_ref[pl.ds(start, 8), 0] = windows.astype(jnp.bfloat16)
        return carry

    lax.fori_loop(0, S // 8, third, 0)

    @pl.when(pl.program_id(0) == pl.num_programs(0) - 1)
    def _():
        for copy in copies:
            copy.wait_recv()
        for copy in copies:
            copy.wait_send()
        gathered_ref[...] = everyone_ref[...]


def turn_lanes(values, sign):
    return pltpu.roll(values, W, 1) * sign


def transform(strips, coords, device_count):
    vmem = pl.BlockSpec(memory_space=pltpu.VMEM)
    facet_local = strips.shape[0]
    whole = lambda *shape: pl.BlockSpec(shape, lambda f: (0,) * len(shape))
    turns = [
        jnp.broadcast_to(table.T[:, :, None], (S, W, 2 * W)) for table in turn_table(W, S, FH)
    ]
    windows, everyone = pl.pallas_call(
        functools.partial(transform_kernel, device_count),
        out_shape=[
            jax.ShapeDtypeStruct((S, facet_local // 2, W, 4 * W), jnp.bfloat16),
            jax.ShapeDtypeStruct((device_count,) + coords.shape, jnp.float32),
        ],
        grid=(facet_local,),
        in_specs=[
            whole(2 * W, W),
            whole(2 * S, S),
            vmem,
            vmem,
            pl.BlockSpec(memory_space=pl.ANY),
            pl.BlockSpec((1, W, S, 2 * W), lambda f: (f, 0, 0, 0)),
        ],
        out_specs=[pl.BlockSpec((S, 1, W, 2 * W), lambda f: (0, f // 2, 0, f % 2)), vmem],
        scratch_shapes=[
            pltpu.VMEM((S, W, 2 * W), jnp.float32),
            pltpu.VMEM((W, S, 2 * W), jnp.float32),
            pltpu.VMEM((device_count,) + coords.shape, jnp.float32),
            pltpu.SemaphoreType.DMA,
            pltpu.SemaphoreType.DMA((device_count - 1,)),
            pltpu.SemaphoreType.DMA((device_count - 1,)),
        ],
        compiler_params=pltpu.CompilerParams(
            vmem_limit_bytes=28 * 2**20, collective_id=0, has_side_effects=True
        ),
        cost_estimate=pl.CostEstimate(
            flops=5 * 10**10, bytes_accessed=64 * 2**20, transcendentals=0
        ),
    )(
        jnp.concatenate(dft_tables(W), axis=0),
        jnp.concatenate(dft_tables(S), axis=0),
        *turns,
        coords,
        strips.reshape(facet_local, W, S, 2 * W),
    )
    return windows.reshape(S, facet_local // 2 * W, 4 * W), everyone


def predict_kernel(
    facet_local, capacity, index_ref, owners_ref, counts_ref, coords_ref, windows_ref, parts_ref,
    out_ref, items_ref, loads_ref
):
    device_count = out_ref.shape[0]
    max_blocks = out_ref.shape[3]
    uppers = facet_local // 2
    scale = 1.0 / (math.sqrt(FH) * SG)
    row_start = ((index_ref[0] * facet_local) // R * W - SG // 2).astype(jnp.float32)
    col_start = ((index_ref[0] * facet_local) % R * W - SG // 2).astype(jnp.float32)
    out_ref[...] = jnp.zeros_like(out_ref)

    def clear(i, carry):
        loads_ref[i] = 0
        return carry

    lax.fori_loop(0, device_count, clear, 0)

    def list_items(s, total):
        owner = owners_ref[s]
        load = loads_ref[owner]
        loads_ref[owner] = load + 1
        place = (s * device_count + owner) * capacity + load

        def add(b, t):
            items_ref[t] = place * max_blocks + b
            return t + 1

        return lax.fori_loop(0, counts_ref[s], add, total)

    total = lax.fori_loop(0, owners_ref.shape[0], list_items, 0)

    def pad(i, carry):
        items_ref[total + i] = items_ref[total - 1]
        return carry

    lax.fori_loop(0, UNROLL - 1, pad, 0)
    lane = out_ref.shape[4]
    ramp = lax.broadcasted_iota(jnp.int32, (8, lane), 0).astype(jnp.float32)

    def one(item):
        b = item % max_blocks
        place = item // max_blocks
        load = place % capacity
        owner = (place // capacity) % device_count
        s = place // (capacity * device_count)
        x = coords_ref[owner, 0, load, pl.ds(b, 1), :]
        y = coords_ref[owner, 1, load, pl.ds(b, 1), :]
        fine = phase(y, ramp)
        upper = phase(y, jnp.where(ramp < uppers, ramp * (2.0 * W) + col_start, 1.0 * W))
        coarse = phase(y, ramp * 8.0)
        coarse = [coarse, twice(coarse, (upper[0][uppers:uppers + 1], upper[1][uppers:uppers + 1]))]
        cos_rows, sin_rows, neg_rows = [], [], []
        for half in coarse:
            c, s_ = half
            cc, ss = twice(
                (c[:, None, :], s_[:, None, :]), (fine[0][None], fine[1][None])
            )
            cos_rows.append(cc.reshape(W, lane).astype(jnp.bfloat16))
            sin_rows.append(ss.reshape(W, lane).astype(jnp.bfloat16))
            neg_rows.append(-sin_rows[-1])
        table = jnp.concatenate(
            [
                jnp.concatenate([cos_rows[0], sin_rows[0], cos_rows[1], sin_rows[1]], axis=0),
                jnp.concatenate([neg_rows[0], cos_rows[0], neg_rows[1], cos_rows[1]], axis=0),
            ],
            axis=1,
        )
        grid = jnp.dot(windows_ref[s], table, preferred_element_type=jnp.float32)
        row_coarse = phase(x, ramp * 8.0 + row_start)
        row_fine = phase(x, ramp)
        sum_real = jnp.zeros((8, lane), jnp.float32)
        sum_imag = jnp.zeros((8, lane), jnp.float32)
        for h in range(uppers):
            mixed = twice((upper[0][h : h + 1], upper[1][h : h + 1]), row_coarse)
            part = grid[h * W : (h + 1) * W].reshape(8, 8, 2 * lane)
            real, imag = part[:, :, :lane], part[:, :, lane:]
            mc, ms = mixed[0][:, None, :], mixed[1][:, None, :]
            sum_real = sum_real + jnp.sum(real * mc + imag * ms, axis=0)
            sum_imag = sum_imag + jnp.sum(imag * mc - real * ms, axis=0)
        fc, fs = row_fine
        vis_real = jnp.sum(sum_real * fc + sum_imag * fs, axis=0, keepdims=True) * scale
        vis_imag = jnp.sum(sum_imag * fc - sum_real * fs, axis=0, keepdims=True) * scale
        return owner, load, b, vis_real, vis_imag

    def step(i, carry):
        for owner, load, b, vis_real, vis_imag in [
            one(items_ref[i * UNROLL + u]) for u in range(UNROLL)
        ]:
            out_ref[owner, load, 0, pl.ds(b, 1), :] = vis_real
            out_ref[owner, load, 1, pl.ds(b, 1), :] = vis_imag
        return carry

    lax.fori_loop(0, (total + UNROLL - 1) // UNROLL, step, 0)
    parts_ref[...] = out_ref[...].astype(jnp.bfloat16)


def predict(windows, owners, counts, coords, device_index):
    device_count, _, capacity, max_blocks, lane = coords.shape
    facet_local = windows.shape[1] // W * 2
    smem = pl.BlockSpec(memory_space=pltpu.SMEM)
    vmem = pl.BlockSpec(memory_space=pltpu.VMEM)
    slots = (device_count, capacity, 2, max_blocks, lane)
    return pl.pallas_call(
        functools.partial(predict_kernel, facet_local, capacity),
        out_shape=jax.ShapeDtypeStruct(slots, jnp.bfloat16),
        in_specs=[smem, smem, smem, vmem, vmem],
        out_specs=vmem,
        scratch_shapes=[
            pltpu.VMEM(slots, jnp.float32),
            pltpu.SMEM((owners.shape[0] * max_blocks + UNROLL,), jnp.int32),
            pltpu.SMEM((device_count,), jnp.int32),
        ],
        compiler_params=pltpu.CompilerParams(vmem_limit_bytes=16 * 2**20),
    )(device_index.reshape(1), owners, counts, coords, windows)


def add_up_kernel(
    device_count, pols, in_ref, out_ref, arrived_ref, total_ref, send_sem, recv_sem, pol_send_sem,
    pol_recv_sem
):
    me = lax.axis_index("fs")
    pol = lax.axis_index("pol")
    peers = [{"fs": lax.rem(me + step, device_count)} for step in range(1, device_count)]
    pol_peers = [{"pol": lax.rem(pol + step, pols)} for step in range(1, pols)]
    barrier = pltpu.get_barrier_semaphore()
    for peer in peers + pol_peers:
        pl.semaphore_signal(
            barrier, inc=1, device_id=peer, device_id_type=pl.DeviceIdType.MESH
        )
    pl.semaphore_wait(barrier, device_count + pols - 2)
    copies = []
    for i, peer in enumerate(peers):
        copy = pltpu.make_async_remote_copy(
            src_ref=in_ref.at[peer["fs"]],
            dst_ref=arrived_ref.at[i],
            send_sem=send_sem.at[i],
            recv_sem=recv_sem.at[i],
            device_id=peer,
            device_id_type=pl.DeviceIdType.MESH,
        )
        copy.start()
        copies.append(copy)
    total_ref[pol] = in_ref[me].astype(jnp.float32)
    for i, copy in enumerate(copies):
        copy.wait_recv()
        total_ref[pol] += arrived_ref[i].astype(jnp.float32)
    pol_copies = []
    for i, peer in enumerate(pol_peers):
        copy = pltpu.make_async_remote_copy(
            src_ref=total_ref.at[pol],
            dst_ref=total_ref.at[pol],
            send_sem=pol_send_sem.at[i],
            recv_sem=pol_recv_sem.at[i],
            device_id=peer,
            device_id_type=pl.DeviceIdType.MESH,
        )
        copy.start()
        pol_copies.append(copy)
    for copy in pol_copies:
        copy.wait_recv()
    for copy in copies + pol_copies:
        copy.wait_send()
    out_ref[...] = total_ref[...]


def add_up(parts, pols):
    device_count = parts.shape[0]
    vmem = pl.BlockSpec(memory_space=pltpu.VMEM)
    return pl.pallas_call(
        functools.partial(add_up_kernel, device_count, pols),
        out_shape=jax.ShapeDtypeStruct((pols,) + parts.shape[1:], jnp.float32),
        in_specs=[vmem],
        out_specs=vmem,
        scratch_shapes=[
            pltpu.VMEM((device_count - 1,) + parts.shape[1:], jnp.bfloat16),
            pltpu.VMEM((pols,) + parts.shape[1:], jnp.float32),
            pltpu.SemaphoreType.DMA((device_count - 1,)),
            pltpu.SemaphoreType.DMA((device_count - 1,)),
            pltpu.SemaphoreType.DMA((pols - 1,)),
            pltpu.SemaphoreType.DMA((pols - 1,)),
        ],
        compiler_params=pltpu.CompilerParams(collective_id=1, has_side_effects=True),
    )(parts)


def correct_kernel(index_ref, owners_ref, counts_ref, left_ref, right_ref, table_ref, vis_ref, out_ref):
    capacity = out_ref.shape[1]
    max_blocks, lane = out_ref.shape[2:]
    chunks = table_ref.shape[1] // lane
    me = index_ref[0]
    out_ref[...] = jnp.zeros_like(out_ref)
    block = lax.broadcasted_iota(jnp.int32, (max_blocks, lane), 0)

    def look_up(first, ids):
        low = ids % lane
        high = ids // lane
        found = []
        for row in range(4):
            entry = None
            for chunk in range(chunks):
                source = jnp.broadcast_to(
                    table_ref[first + row : first + row + 1, chunk * lane : (chunk + 1) * lane],
                    (max_blocks, lane),
                )
                got = jnp.take_along_axis(source, low, axis=1, mode="promise_in_bounds")
                entry = got if entry is None else jnp.where(high == chunk, got, entry)
            found.append(entry)
        return [(found[0], found[1]), (found[2], found[3])]

    def product(a, b):
        return (a[0] * b[0] - a[1] * b[1], a[0] * b[1] + a[1] * b[0])

    def slot(s, load):
        is_mine = owners_ref[s] == me

        @pl.when(is_mine)
        def _():
            left = look_up(0, left_ref[load])
            right = look_up(4, right_ref[load])
            total_real = jnp.zeros((max_blocks, lane), jnp.float32)
            total_imag = jnp.zeros((max_blocks, lane), jnp.float32)
            for inner_row in range(2):
                for inner_col in range(2):
                    comp = 2 * inner_row + inner_col
                    step = product(
                        left[inner_row], (vis_ref[comp, load, 0], vis_ref[comp, load, 1])
                    )
                    step = product(step, (right[inner_col][0], -right[inner_col][1]))
                    total_real = total_real + step[0]
                    total_imag = total_imag + step[1]
            keep = block < counts_ref[s]
            out_ref[0, load] = jnp.where(keep, total_real, 0.0)
            out_ref[1, load] = jnp.where(keep, total_imag, 0.0)

        return load + is_mine.astype(jnp.int32)

    lax.fori_loop(0, owners_ref.shape[0], slot, 0)


def correct(visible, owners, counts, station_ids, tables, device_index):
    _, capacity, _, max_blocks, lane = visible.shape
    smem = pl.BlockSpec(memory_space=pltpu.SMEM)
    vmem = pl.BlockSpec(memory_space=pltpu.VMEM)
    return pl.pallas_call(
        correct_kernel,
        out_shape=jax.ShapeDtypeStruct((2, capacity, max_blocks, lane), jnp.float32),
        in_specs=[smem, smem, smem, vmem, vmem, vmem, vmem],
        out_specs=vmem,
    )(
        device_index.reshape(1),
        owners,
        counts,
        station_ids[:, :, 0, :],
        station_ids[:, :, 1, :],
        tables,
        visible,
    )


def on_device(facets, owners, counts, coords, station_ids, jones_table):
    device_index = lax.axis_index("fs").astype(jnp.int32)
    pol_index = lax.axis_index("pol")
    device_count, pols = lax.axis_size("fs"), lax.axis_size("pol")
    windows, all_coords = transform(facets[0], coords, device_count)
    visible = add_up(predict(windows, owners, counts, all_coords, device_index), pols)
    tables = jnp.concatenate(
        [
            lax.dynamic_slice_in_dim(jones_table, 4 * (pol_index // 2), 4, 0),
            lax.dynamic_slice_in_dim(jones_table, 4 * (pol_index % 2), 4, 0),
        ],
        axis=0,
    )
    return correct(visible, owners, counts, station_ids, tables, device_index)[None]


def solution(mesh):
    return jax.shard_map(
        on_device,
        mesh=mesh,
        in_specs=(
            P("pol", "fs", None, None),
            P(),
            P(),
            P(None, "fs", None, None),
            P("fs", None, None, None),
            P(),
        ),
        out_specs=P("pol", None, "fs", None, None),
        check_vma=False,
    )
```
